32 devices in a mesh: scan: 4 (over x, core), pix: 8 (over z, y).
Axes of the slice: x: 2, y: 2, z: 4, core: 2. Of those that a mesh axis runs over, the one named last changes fastest.
Arguments:
- raw_frames: float32 [1536, 128, 128], P(('scan', 'pix')), may hold values from 0.2 to 5
- gain_map: float32 [128, 128], replicated, may hold values from 0.5 to 1.5
- coupling: float32 [128, 128], replicated, may hold values from 0.05 to 0.25
- factor_w: float32 [1536, 256], P(('scan', 'pix')), may hold values from 0.01 to 0.25
- factor_h: float32 [256, 16384], P('scan', 'pix'), may hold values from 0.01 to 0.25
Outputs:
- w_factor: float32 [1536, 256], P(('scan', 'pix'))
- h_factor: float32 [256, 16384], P('scan', 'pix')
The draws below stay inside these ranges and needn't reach their ends.
All inputs are finite; a program needn't handle non-finite values.
Results may differ from the reference program's by a relative error of at most 0.0003.
Values may be sent and summed in bfloat16 or wider, within the bound.
No kernel may reach another device: no remote copies, remote signals or barrier semaphores. Data moves between devices by JAX's collectives and lax.ppermute only.
A program may use at most 64 MiB of HBM per device.

```python
import math
import jax
import jax.numpy as jnp
from jax import lax

FRAME = 128
RANK = 256
SWEEPS = 4
ITERS = 2
FR_DEV = 48
FRAMES = 1536
PIXELS = 16384
N_SCAN = 4
N_PIX = 8


def shard_levels(rng, extent, shards, smallest, top_value):
    level = 1.0
    for position, shards_of in shards:
        draws = jax.random.uniform(jax.random.fold_in(jax.random.fold_in(rng, 6), position), (shards_of,), jnp.float32, smallest / len(shards), top_value / len(shards))
        level = level * jnp.repeat(jnp.exp(draws), extent[position] // shards_of).reshape((-1,) + (1,) * (len(extent) - 1 - position))
    return level


def setup_inputs(seed: int = 0) -> dict:
    streams_of = jax.random.split(jax.random.key(seed), 6)
    raw_frames = jnp.clip(jnp.exp(math.log(5.0) - 3.218876 * jax.random.uniform(streams_of[0], (FRAMES, FRAME, FRAME), jnp.float32) ** shard_levels(streams_of[0], (FRAMES, FRAME, FRAME), ((0, 32),), -0.2, 0.2)), 0.2, 5.0)
    gain_map = jnp.clip(1.0 + 0.1 * jax.random.normal(streams_of[1], (FRAME, FRAME), jnp.float32), 0.5, 1.5)
    coupling = jnp.clip(jnp.exp(jax.random.uniform(streams_of[2], (FRAME, FRAME), jnp.float32, math.log(0.05), math.log(0.25))), 0.05, 0.25)
    factor_w = jnp.clip(jnp.exp(math.log(0.25) - 3.218876 * jax.random.uniform(streams_of[3], (FRAMES, RANK), jnp.float32) ** shard_levels(streams_of[3], (FRAMES, RANK), ((0, 32),), -0.2, 0.2)), 0.01, 0.25)
    factor_h = jnp.clip(jnp.exp(math.log(0.25) - 3.218876 * jax.random.uniform(streams_of[4], (RANK, PIXELS), jnp.float32) ** shard_levels(streams_of[4], (RANK, PIXELS), ((0, 4), (1, 8)), -0.2, 0.2)), 0.01, 0.25)
    return dict(raw_frames=raw_frames, gain_map=gain_map, coupling=coupling, factor_w=factor_w, factor_h=factor_h)


def stencil(frames, gain_map, coupling):
    measured = frames * gain_map[None]
    charge = measured
    for sweep in range(SWEEPS):
        padded = jnp.pad(charge, ((0, 0), (1, 1), (1, 1)))
        neighbours = padded[:, 2:, 1:-1] + padded[:, :-2, 1:-1] + padded[:, 1:-1, 2:] + padded[:, 1:-1, :-2]
        charge = (measured + coupling[None] * neighbours) / (1.0 + 4.0 * coupling[None])
    return charge.reshape(frames.shape[0], -1)


def reference(raw_frames, gain_map, coupling, factor_w, factor_h):
    block_rows = FR_DEV * N_PIX
    blocks = raw_frames.reshape(N_SCAN, block_rows, FRAME, FRAME)
    tile_data = lax.map(lambda frames: stencil(frames, gain_map, coupling), blocks)
    w_blocks = factor_w.reshape(N_SCAN, block_rows, RANK)
    h_full = factor_h
    for rounds in range(ITERS):
        h_round = h_full.astype(jnp.bfloat16)
        h_sums = jnp.sum(h_round.astype(jnp.float32), axis=1)

        def w_update(pair):
            values, w_block = pair
            w_round = w_block.astype(jnp.bfloat16)
            product = jnp.dot(w_round, h_round, preferred_element_type=jnp.float32)
            count_ratio = (values / product).astype(jnp.bfloat16)
            numerator = jnp.dot(count_ratio, h_round.T, preferred_element_type=jnp.float32)
            return w_block * numerator / h_sums

        w_blocks = lax.map(w_update, (tile_data, w_blocks))
        w_round_all = w_blocks.astype(jnp.bfloat16)
        w_sums = jnp.sum(w_round_all.astype(jnp.float32), axis=(0, 1))

        def h_term(pair):
            values, w_round = pair
            product = jnp.dot(w_round, h_round, preferred_element_type=jnp.float32)
            count_ratio = (values / product).astype(jnp.bfloat16)
            return lax.dot_general(w_round, count_ratio, (((0,), (0,)), ((), ())), preferred_element_type=jnp.float32)

        numerator_h = jnp.sum(lax.map(h_term, (tile_data, w_round_all)), axis=0)
        h_full = h_full * numerator_h / w_sums[:, None]
    return w_blocks.reshape(N_SCAN * block_rows, RANK), h_full
```

```python
import functools

import jax
import jax.numpy as jnp
from jax import lax
from jax.experimental import pallas as pl
from jax.experimental.pallas import tpu as pltpu
from jax.sharding import PartitionSpec as P

SWEEPS = 4
ITERS = 2
BF16, F16, F32 = jnp.bfloat16, jnp.float16, jnp.float32


def stencil_body(me_ref, raw_ref, gain_ref, couple_ref, out_ref):
    group, rows, cols = raw_ref.shape
    parts = out_ref.shape[0]
    band = rows // parts
    lane = lax.broadcasted_iota(jnp.int32, (group, cols), 1)
    has_left = jnp.where(lane == 0, 0.0, 1.0)
    has_right = jnp.where(lane == cols - 1, 0.0, 1.0)
    scaled = {}
    weight = {}
    level = [dict() for _ in range(SWEEPS + 1)]
    for step in range(rows + SWEEPS):
        if step < rows:
            gain = gain_ref[step : step + 1, :]
            couple = couple_ref[step : step + 1, :]
            inverse = 1.0 / (1.0 + 4.0 * couple)
            measured = raw_ref[:, step, :] * gain
            level[0][step] = measured
            scaled[step] = measured * inverse
            weight[step] = couple * inverse
        for sweep in range(1, SWEEPS + 1):
            row = step - sweep
            if row < 0 or row >= rows:
                continue
            old = level[sweep - 1]
            centre = old[row]
            near = pltpu.roll(centre, 1, 1) * has_left + pltpu.roll(centre, cols - 1, 1) * has_right
            if row > 0:
                near = near + old[row - 1]
            if row < rows - 1:
                near = near + old[row + 1]
            value = scaled[row] + weight[row] * near
            if sweep < SWEEPS:
                level[sweep][row] = value
            else:
                part = jnp.bitwise_xor(me_ref[0], row // band)
                start = (row % band) * cols
                out_ref[part, :, start : start + cols] = value


def correct(raw_frames, gain_map, coupling, me, parts):
    frames, rows, cols = raw_frames.shape
    group = 8
    pixels = rows * cols // parts
    return pl.pallas_call(
        stencil_body,
        out_shape=jax.ShapeDtypeStruct((parts, frames, pixels), F32),
        grid_spec=pltpu.PrefetchScalarGridSpec(
            num_scalar_prefetch=1,
            grid=(frames // group,),
            in_specs=[
                pl.BlockSpec((group, rows, cols), lambda i, m: (i, 0, 0)),
                pl.BlockSpec((rows, cols), lambda i, m: (0, 0)),
                pl.BlockSpec((rows, cols), lambda i, m: (0, 0)),
            ],
            out_specs=pl.BlockSpec((parts, group, pixels), lambda i, m: (0, i, 0)),
        ),
        cost_estimate=pl.CostEstimate(
            flops=frames * rows * cols * SWEEPS * 9,
            bytes_accessed=frames * rows * cols * 8,
            transcendentals=0,
        ),
        name="charge_sharing",
    )(me[None].astype(jnp.int32), raw_frames, gain_map, coupling)


def relative(blocks, index, bits):
    for bit in range(bits):
        flip = (index >> bit) & 1
        blocks = [jnp.where(flip == 1, blocks[j ^ (1 << bit)], blocks[j]) for j in range(len(blocks))]
    return blocks


def halves(value):
    high = value.astype(F16)
    return high, (value - high.astype(F32)).astype(F16)


def local(raw_frames, gain_map, coupling, factor_w, factor_h, n_scan, n_pix):
    scan_bits, pix_bits = n_scan.bit_length() - 1, n_pix.bit_length() - 1
    scan = lax.axis_index("scan")
    me = lax.axis_index("pix")
    row_count, rank = factor_w.shape
    comp_rows, pixels = factor_h.shape
    half = rank // 2
    x_bits = [1 << b for b in range(1, scan_bits)]
    gather_bits = [1 << b for b in range(1, pix_bits)] + [1]

    def over_pix(value, bit):
        return lax.ppermute(value, "pix", [(i, i ^ bit) for i in range(n_pix)])

    def over_scan(value, bit):
        return lax.ppermute(value, "scan", [(i, i ^ bit) for i in range(n_scan)])

    comp_order = [2 * j + c for c in range(2) for j in range(n_scan // 2)]

    def to_local(w):
        blocks = relative([w[:, comp_rows * j : comp_rows * (j + 1)] for j in range(n_scan)], scan, scan_bits)
        return jnp.concatenate([blocks[j] for j in comp_order], axis=1)

    def to_global(w):
        at = {j: w[:, comp_rows * i : comp_rows * (i + 1)] for i, j in enumerate(comp_order)}
        return jnp.concatenate(relative([at[j] for j in range(n_scan)], scan, scan_bits), axis=1)

    h_list = [factor_h]
    for bit in x_bits:
        got = over_scan(jnp.concatenate(h_list, 0), bit)
        h_list = h_list + [got[comp_rows * i : comp_rows * (i + 1)] for i in range(len(h_list))]
    h_own = jnp.concatenate(h_list, 0)

    w_local = to_local(factor_w)
    w_first = w_local.astype(BF16)

    data = correct(raw_frames, gain_map, coupling, me, n_pix)
    order = [0]
    for bit in gather_bits:
        order = order + [r | bit for r in order]
    far_first = sorted(range(1, n_pix), reverse=True)
    got = {}
    for r in far_first:
        block = jnp.concatenate([data[r], w_first.astype(F32)], axis=1).astype(F16)
        got[r] = over_pix(block, r)
    tile = {r: got[r][:, :pixels] for r in far_first}
    tile[0] = data[0].astype(F16)
    w_rows = {r: got[r][:, pixels:].astype(BF16) for r in far_first}
    w_rows[0] = w_first

    for rounds in range(ITERS):
        h_mine = h_own.astype(BF16)
        h_block = jnp.concatenate([h_mine, over_scan(h_mine, 1)], axis=0)
        h_part = jnp.sum(h_block.astype(F32), axis=1)

        def numerator_of(values, w_round):
            product = jnp.dot(w_round, h_block, preferred_element_type=F32)
            ratio = (values.astype(F32) / product).astype(BF16)
            return lax.dot_general(ratio, h_block, (((1,), (1,)), ((), ())), preferred_element_type=F32)

        if rounds == 0:
            high, low = halves(h_part)
            sums = jnp.concatenate([high[None], low[None], jnp.zeros((14, rank), F16)], axis=0)
            numerator = numerator_of(tile[0], w_rows[0])
            h_sums = h_part
            for r in far_first:
                mean = (numerator_of(tile[r], w_rows[r]) / h_part).astype(F16)
                back = over_pix(jnp.concatenate([mean, sums], axis=0), r).astype(F32)
                weight = back[row_count] + back[row_count + 1]
                numerator = numerator + back[:row_count] * weight
                h_sums = h_sums + weight
            data_all = jnp.concatenate([tile[r] for r in order], axis=0)
        else:
            rows = data_all.shape[0] // 2
            away = numerator_of(data_all[rows:], w_all[rows:])
            near = numerator_of(data_all[:rows], w_all[:rows])
            h_sums = h_part
            for bit in gather_bits[::-1]:
                rows = near.shape[0]
                wire = F32 if rows == row_count else F16
                high, low = halves(h_sums)
                sums = jnp.concatenate([high[None], low[None], jnp.zeros((14, rank), F16)], axis=0)
                message = jnp.concatenate([(away / h_sums).astype(wire), sums.astype(wire)], axis=0)
                back = over_pix(message, bit).astype(F32)
                weight = back[rows] + back[rows + 1]
                near = near + back[:rows] * weight
                h_sums = h_sums + weight
                numerator, away, near = near, near[rows // 2 :], near[: rows // 2]
        w_local = w_local * numerator / h_sums

        w_all = w_local.astype(BF16)
        for bit in gather_bits:
            w_all = jnp.concatenate([w_all, over_pix(w_all, bit)], axis=0)
        w_part = jnp.sum(w_all.astype(F32), axis=0)
        product = jnp.dot(w_all, h_block, preferred_element_type=F32)
        ratio = (data_all.astype(F32) / product).astype(BF16)
        total = lax.dot_general(w_all, ratio, (((0,), (0,)), ((), ())), preferred_element_type=F32)
        w_sums = w_part[:half] + over_scan(w_part[half:], 1)
        total = total[:half] + over_scan(total[half:], 1)
        last = rounds == ITERS - 1
        for bit in x_bits[::-1]:
            blocks = total.shape[0] // comp_rows
            step = bit >> 1
            if last:
                keep = [i for i in range(blocks) if not i & step]
                send = [i | step for i in keep]
            else:
                keep = list(range(blocks))
                send = [i ^ step for i in keep]

            def pick(value, which):
                return jnp.concatenate([value[comp_rows * i : comp_rows * (i + 1)] for i in which], axis=0)

            sums = pick(w_sums, send)
            high, low = halves(sums)
            tail = jnp.concatenate([high[:, None], low[:, None], jnp.zeros((len(sums), 126), F16)], axis=1)
            message = jnp.concatenate([(pick(total, send) / sums[:, None]).astype(F16), tail], axis=1)
            back = over_scan(message, bit).astype(F32)
            weight = back[:, pixels] + back[:, pixels + 1]
            total = pick(total, keep) + back[:, :pixels] * weight[:, None]
            w_sums = pick(w_sums, keep) + weight
        h_own = h_own[: total.shape[0]] * total / w_sums[:, None]
    return (to_global(w_local), h_own)


def solution(mesh):
    return jax.shard_map(
        functools.partial(local, n_scan=mesh.shape["scan"], n_pix=mesh.shape["pix"]),
        mesh=mesh,
        in_specs=(
            P(("scan", "pix"), None, None),
            P(),
            P(),
            P(("scan", "pix"), None),
            P("scan", "pix"),
        ),
        out_specs=(P(("scan", "pix"), None), P("scan", "pix")),
        check_vma=False,
    )
```

```python
import functools

import jax
import jax.numpy as jnp
from jax import lax
from jax.experimental import pallas as pl
from jax.experimental.pallas import tpu as pltpu
from jax.sharding import PartitionSpec as P

SWEEPS = 4
ITERS = 2
BF16, F16, F32 = jnp.bfloat16, jnp.float16, jnp.float32


def stencil_body(me_ref, raw_ref, gain_ref, couple_ref, w_ref, *refs):
    out_refs, (gain_s, near_s, stage) = refs[:-3], refs[-3:]
    rows, cols = gain_ref.shape
    parts, frames, pixels = stage.shape
    groups = frames // 8
    band = rows // parts

    @pl.when(pl.program_id(0) == 0)
    def _():
        inverse = 1.0 / (1.0 + 4.0 * couple_ref[...])
        gain_s[...] = gain_ref[...] * inverse
        near_s[...] = couple_ref[...] * inverse

    lane = lax.broadcasted_iota(jnp.int32, (8, cols), 1)
    has_left = jnp.where(lane == 0, 0.0, 1.0)
    has_right = jnp.where(lane == cols - 1, 0.0, 1.0)
    zero = jnp.zeros((8, cols), F32)

    def every(ref, row):
        return ref[pl.ds(row, 8, stride=0), :]

    def advance(state, row, end=False):
        levels, scaled, weight = state
        if end:
            w_new = zero
            enter = [zero] * groups
            s_new = [zero] * groups
        else:
            w_new = every(near_s, row)
            gain = every(gain_ref, row)
            gain_scaled = every(gain_s, row)
            raws = [raw_ref[pl.ds(g * 8 * rows + row, 8, stride=rows), :] for g in range(groups)]
            enter = [raw * gain for raw in raws]
            s_new = [raw * gain_scaled for raw in raws]
        out, new_levels = [], []
        for g in range(groups):
            new = enter[g]
            mine = []
            for k in range(SWEEPS):
                older, newer = levels[g][k]
                side = pltpu.roll(newer, 1, 1) * has_left + pltpu.roll(newer, cols - 1, 1) * has_right
                value = scaled[g][k] + weight[k] * ((older + side) + new)
                mine.append((newer, new))
                new = value
            out.append(new)
            new_levels.append(mine)
        scaled = [[s_new[g]] + scaled[g][: SWEEPS - 1] for g in range(groups)]
        return (new_levels, scaled, [w_new] + weight[: SWEEPS - 1]), out

    frame = lax.broadcasted_iota(jnp.int32, (frames, cols), 0) + frames * pl.program_id(0)
    phase = frame.astype(F32) * 0.6180340 + lax.broadcasted_iota(jnp.int32, (frames, cols), 1).astype(F32) * 0.7548777
    shift = (phase - jnp.floor(phase) - 0.5) * 0.005

    def one_band(part, state, error, first=False, last=False):
        for i in range(band):
            state, out = advance(state, part * band + SWEEPS + i, end=last and i + SWEEPS >= band)
            value = jnp.concatenate(out, axis=0)
            value = value + (value * shift if first and i == 0 else error)
            rounded = value.astype(BF16)
            error = value - rounded.astype(F32)
            stage[part, :, i * cols : (i + 1) * cols] = rounded
        return state, error

    state = (
        [[(zero, zero)] * SWEEPS for _ in range(groups)],
        [[zero] * SWEEPS for _ in range(groups)],
        [zero] * SWEEPS,
    )
    for row in range(SWEEPS):
        state, _ = advance(state, row)
    carry = one_band(0, state, None, first=True)
    carry = lax.fori_loop(1, parts - 1, lambda part, c: one_band(part, *c), carry)
    one_band(parts - 1, *carry, last=True)
    w_mine = w_ref[...].astype(BF16)
    for r, out_ref in enumerate(out_refs):
        out_ref[:, :pixels] = stage[jnp.bitwise_xor(me_ref[0], r)]
        out_ref[:, pixels:] = w_mine


def correct(raw_frames, gain_map, coupling, w_local, me, parts, start, count):
    frames, rows, cols = raw_frames.shape
    rank = w_local.shape[1]
    group = 16
    pixels = rows * cols // parts
    first = start // group
    return pl.pallas_call(
        stencil_body,
        out_shape=[jax.ShapeDtypeStruct((count, pixels + rank), BF16)] * parts,
        grid_spec=pltpu.PrefetchScalarGridSpec(
            num_scalar_prefetch=1,
            grid=(count // group,),
            in_specs=[
                pl.BlockSpec((group * rows, cols), lambda i, m: (i + first, 0)),
                pl.BlockSpec((rows, cols), lambda i, m: (0, 0)),
                pl.BlockSpec((rows, cols), lambda i, m: (0, 0)),
                pl.BlockSpec((group, rank), lambda i, m: (i + first, 0)),
            ],
            out_specs=[pl.BlockSpec((group, pixels + rank), lambda i, m: (i, 0))] * parts,
            scratch_shapes=[pltpu.VMEM((rows, cols), F32)] * 2 + [pltpu.VMEM((parts, group, pixels), BF16)],
        ),
        cost_estimate=pl.CostEstimate(
            flops=count * rows * cols * SWEEPS * 9,
            bytes_accessed=count * rows * cols * 6,
            transcendentals=0,
        ),
        name="charge_sharing",
    )(me[None].astype(jnp.int32), raw_frames.reshape(frames * rows, cols), gain_map, coupling, w_local)


TILE = 256


def ratio_tile(data_refs, w, h_refs, at, tile):
    h_tile = jnp.concatenate([ref[:, at : at + tile] for ref in h_refs], axis=0)
    product = jnp.dot(w, h_tile, preferred_element_type=F32)
    values = jnp.concatenate([ref[:, at : at + tile] for ref in data_refs], axis=0).astype(F32)
    return (values / product).astype(BF16), h_tile


def rows_of(data_refs, pixels):
    return jnp.concatenate([ref[:, pixels:] for ref in data_refs], axis=0)


def w_term_body(*refs):
    *data_refs, h_one, h_two, out_ref = refs
    pixels = h_one.shape[1]
    w = rows_of(data_refs, pixels)
    tile = min(TILE, pixels)
    total = None
    for at in range(0, pixels, tile):
        ratio, h_tile = ratio_tile(data_refs, w, (h_one, h_two), at, tile)
        term = lax.dot_general(ratio, h_tile, (((1,), (1,)), ((), ())), preferred_element_type=F32)
        total = term if total is None else total + term
    out_ref[...] = total


def tiles_body(*refs):
    *data_refs, out_ref = refs
    pixels = out_ref.shape[1]
    row = 0
    for ref in data_refs:
        out_ref[row : row + ref.shape[0], :] = ref[:, :pixels]
        row += ref.shape[0]


VMEM = pl.BlockSpec(memory_space=pltpu.VMEM)


def term(body, out_shape, args, flops):
    single = not isinstance(out_shape, list)
    return pl.pallas_call(
        body,
        out_shape=out_shape,
        in_specs=[VMEM] * len(args),
        out_specs=VMEM if single else [VMEM] * len(out_shape),
        cost_estimate=pl.CostEstimate(flops=flops, bytes_accessed=sum(a.size * 2 for a in args), transcendentals=0),
    )(*args)


def relative(blocks, index, bits):
    for bit in range(bits):
        flip = (index >> bit) & 1
        blocks = [jnp.where(flip == 1, blocks[j ^ (1 << bit)], blocks[j]) for j in range(len(blocks))]
    return blocks


def halves(value):
    high = value.astype(F16)
    return high, (value - high.astype(F32)).astype(F16)


def with_sums(block, sums):
    high, low = halves(sums)
    return jnp.concatenate([block.astype(F16), high[None], low[None], jnp.zeros((14, len(sums)), F16)], axis=0)


def chunks_of(frames):
    return [(0, frames - 16), (frames - 16, 16)] if frames > 16 else [(0, frames)]


def groups_of(n_pix):
    near = list(range(n_pix // 2))
    far = list(range(n_pix - 1, n_pix // 2 - 1, -1))
    return [near] + [far[i : i + 2] for i in range(0, len(far), 2)]


def local(raw_frames, gain_map, coupling, factor_w, factor_h, n_scan, n_pix):
    scan_bits = n_scan.bit_length() - 1
    scan = lax.axis_index("scan")
    me = lax.axis_index("pix")
    row_count, rank = factor_w.shape
    comp_rows, pixels = factor_h.shape
    half = rank // 2
    x_bits = [1 << b for b in range(1, scan_bits)]
    far = list(range(2, n_pix, 2))
    even = [0] + far
    odd = [r + 1 for r in even]
    scale = 1.0 / (pixels // 8)

    def over_pix(value, bit):
        return lax.ppermute(value, "pix", [(i, i ^ bit) for i in range(n_pix)])

    def over_scan(value, bit):
        return lax.ppermute(value, "scan", [(i, i ^ bit) for i in range(n_scan)])

    comp_order = [2 * j + c for c in range(2) for j in range(n_scan // 2)]

    def to_local(w):
        blocks = relative([w[:, comp_rows * j : comp_rows * (j + 1)] for j in range(n_scan)], scan, scan_bits)
        return jnp.concatenate([blocks[j] for j in comp_order], axis=1)

    def to_global(w):
        at = {j: w[:, comp_rows * i : comp_rows * (i + 1)] for i, j in enumerate(comp_order)}
        return jnp.concatenate(relative([at[j] for j in range(n_scan)], scan, scan_bits), axis=1)

    w_local = to_local(factor_w)

    tile = {r: [] for r in range(n_pix)}
    for start, count in chunks_of(raw_frames.shape[0]):
        messages = correct(raw_frames, gain_map, coupling, w_local, me, n_pix, start, count)
        for r in range(n_pix - 1, 0, -1):
            tile[r].append(over_pix(messages[r], r))
        tile[0].append(messages[0])

    h_own = factor_h
    for bit in x_bits:
        h_own = jnp.concatenate([h_own, over_scan(h_own, bit)], 0)

    def blocks(which):
        return [part for r in which for part in tile[r]]

    for rounds in range(ITERS):
        h_mine = h_own.astype(BF16)
        h_pair = [h_mine, over_scan(h_mine, 1)]
        h_part = jnp.concatenate([jnp.sum(h.astype(F32), axis=1) for h in h_pair])

        def numerator_of(values, w_round):
            h_block = jnp.concatenate(h_pair, axis=0)
            product = jnp.dot(w_round, h_block, preferred_element_type=F32)
            ratio = (values.astype(F32) / product).astype(BF16)
            return lax.dot_general(ratio, h_block, (((1,), (1,)), ((), ())), preferred_element_type=F32)

        if rounds == 0:
            backs = []
            for group in groups_of(n_pix):
                rows = row_count * len(group)
                out = jax.ShapeDtypeStruct((rows, rank), F32)
                partial = term(w_term_body, out, blocks(group) + h_pair, 4 * rows * rank * pixels) * scale
                for j, r in enumerate(group):
                    block = partial[row_count * j : row_count * (j + 1)]
                    if r == 0:
                        numerator = block
                    else:
                        backs.append(over_pix(with_sums(block, h_part * scale), r))
            everything = functools.reduce(lambda a, b: a + b, [b.astype(F32) for b in backs])
            numerator = numerator + everything[:row_count]
            h_sums = h_part * scale + everything[row_count] + everything[row_count + 1]
        else:
            rows = row_count * len(even)
            away = numerator_of(data_all[rows:], w_odd)
            back = over_pix(with_sums(away / h_part - 1.0, h_part), 1)
            near = numerator_of(data_all[:rows], w_even)
            weight = back[rows].astype(F32) + back[rows + 1].astype(F32)
            near = near + (back[:rows].astype(F32) + 1.0) * weight
            h_two = h_part + weight
            numerator, h_sums = near[:row_count], h_two
            for i, r in enumerate(far):
                mean = near[row_count * (i + 1) : row_count * (i + 2)] / h_two - 1.0
                back = over_pix(with_sums(mean, h_two), r)
                weight = back[row_count].astype(F32) + back[row_count + 1].astype(F32)
                numerator = numerator + (back[:row_count].astype(F32) + 1.0) * weight
                h_sums = h_sums + weight
        w_local = w_local * numerator / h_sums

        w_mine = w_local.astype(BF16)
        w_even = jnp.concatenate([w_mine] + [over_pix(w_mine, r) for r in far], axis=0)
        w_odd = over_pix(w_even, 1)
        if rounds == 0:
            shape = jax.ShapeDtypeStruct((row_count * n_pix, pixels), BF16)
            data_all = term(tiles_body, shape, blocks(even + odd), 0)
        w_all = jnp.concatenate([w_even, w_odd], axis=0)
        w_part = jnp.sum(w_all.astype(F32), axis=0)
        last = rounds == ITERS - 1
        w_sums = w_part[:half] + over_scan(w_part[half:], 1)
        product = jnp.dot(w_all, jnp.concatenate(h_pair, axis=0), preferred_element_type=F32)
        ratio = (data_all.astype(F32) / product).astype(BF16)

        def numerator_rows(w):
            return lax.dot_general(w, ratio, (((0,), (0,)), ((), ())), preferred_element_type=F32)

        other = over_scan(numerator_rows(w_all[:, half:]), 1)
        total = numerator_rows(w_all[:, :half]) + other
        for bit in x_bits[::-1]:
            count = total.shape[0] // comp_rows
            step = bit >> 1
            if last:
                keep = [i for i in range(count) if not i & step]
                send = [i | step for i in keep]
            else:
                keep = list(range(count))
                send = [i ^ step for i in keep]

            def pick(value, which):
                if list(which) == list(range(which[0], which[0] + len(which))):
                    return value[comp_rows * which[0] : comp_rows * (which[-1] + 1)]
                return jnp.concatenate([value[comp_rows * i : comp_rows * (i + 1)] for i in which], axis=0)

            sums = pick(w_sums, send)
            weight = over_scan(sums, bit)
            message = (pick(total, send) / sums[:, None] - 1.0).astype(F16)
            back = over_scan(message, bit).astype(F32) + 1.0
            total = pick(total, keep) + back * weight[:, None]
            w_sums = pick(w_sums, keep) + weight
        h_own = h_own[: total.shape[0]] * total / w_sums[:, None]
    return (to_global(w_local), h_own)


def solution(mesh):
    n_pix = mesh.shape["pix"]

    def layer(*args):
        return local(*args, n_scan=mesh.shape["scan"], n_pix=n_pix)

    return jax.shard_map(
        layer,
        mesh=mesh,
        in_specs=(
            P(("scan", "pix"), None, None),
            P(),
            P(),
            P(("scan", "pix"), None),
            P("scan", "pix"),
        ),
        out_specs=(P(("scan", "pix"), None), P("scan", "pix")),
        check_vma=False,
    )
```

```python
import functools

import jax
import jax.numpy as jnp
from jax import lax
from jax.experimental import pallas as pl
from jax.experimental.pallas import tpu as pltpu
from jax.sharding import PartitionSpec as P

SWEEPS = 4
ITERS = 2
BF16, F16, F32 = jnp.bfloat16, jnp.float16, jnp.float32


def relative(blocks, index):
    for bit in range(len(blocks).bit_length() - 1):
        flip = (index >> bit) & 1
        blocks = [jnp.where(flip == 1, blocks[j ^ (1 << bit)], blocks[j]) for j in range(len(blocks))]
    return blocks


def reordered(w, index, order):
    width = w.shape[1] // len(order)
    blocks = relative([w[:, width * j : width * (j + 1)] for j in range(len(order))], index)
    return jnp.concatenate([blocks[j] for j in order], axis=1)


def stencil_body(me_ref, raw_ref, gain_ref, couple_ref, *refs, start, order, near):
    refs, (gain_s, near_s, stage) = refs[:-3], refs[-3:]
    rows, cols = gain_ref.shape
    parts, frames, pixels = stage.shape
    groups = frames // 8
    band = rows // parts

    @pl.when(pl.program_id(0) == 0)
    def _():
        inverse = 1.0 / (1.0 + 4.0 * couple_ref[...])
        gain_s[...] = gain_ref[...] * inverse
        near_s[...] = couple_ref[...] * inverse

    lane = lax.broadcasted_iota(jnp.int32, (8, cols), 1)
    has_left = jnp.where(lane == 0, 0.0, 1.0)
    has_right = jnp.where(lane == cols - 1, 0.0, 1.0)
    zero = jnp.zeros((8, cols), F32)

    def every(ref, row):
        return ref[pl.ds(row, 8, stride=0), :]

    def advance(state, row, end=False):
        levels, scaled, weight = state
        if end:
            w_new = zero
            enter = [zero] * groups
            s_new = [zero] * groups
        else:
            w_new = every(near_s, row)
            gain = every(gain_ref, row)
            gain_scaled = every(gain_s, row)
            raws = [raw_ref[pl.ds(g * 8 * rows + row, 8, stride=rows), :] for g in range(groups)]
            enter = [raw * gain for raw in raws]
            s_new = [raw * gain_scaled for raw in raws]
        out, new_levels = [], []
        for g in range(groups):
            new = enter[g]
            mine = []
            for k in range(SWEEPS):
                older, newer = levels[g][k]
                side = pltpu.roll(newer, 1, 1) * has_left + pltpu.roll(newer, cols - 1, 1) * has_right
                value = scaled[g][k] + weight[k] * ((older + side) + new)
                mine.append((newer, new))
                new = value
            out.append(new)
            new_levels.append(mine)
        scaled = [[s_new[g]] + scaled[g][: SWEEPS - 1] for g in range(groups)]
        return (new_levels, scaled, [w_new] + weight[: SWEEPS - 1]), out

    frame = lax.broadcasted_iota(jnp.int32, (frames, cols), 0) + frames * pl.program_id(0) + start
    phase = frame.astype(F32) * 0.6180340 + lax.broadcasted_iota(jnp.int32, (frames, cols), 1).astype(F32) * 0.7548777
    shift = (phase - jnp.floor(phase) - 0.5) * 0.005

    def one_band(part, state, error, first=False, last=False):
        for i in range(band):
            state, out = advance(state, part * band + SWEEPS + i, end=last and i + SWEEPS >= band)
            value = jnp.concatenate(out, axis=0)
            value = value + (value * shift if first and i == 0 else error)
            rounded = value.astype(BF16)
            error = value - rounded.astype(F32)
            stage[part, :, i * cols : (i + 1) * cols] = rounded
        return state, error

    state = (
        [[(zero, zero)] * SWEEPS for _ in range(groups)],
        [[zero] * SWEEPS for _ in range(groups)],
        [zero] * SWEEPS,
    )
    for row in range(SWEEPS):
        state, _ = advance(state, row)
    carry = one_band(0, state, None, first=True)
    carry = lax.fori_loop(1, parts - 1, lambda part, c: one_band(part, *c), carry)
    one_band(parts - 1, *carry, last=True)

    def mine(r):
        return stage[jnp.bitwise_xor(me_ref[0], r)]

    if near is None:
        for r, out_ref in enumerate(refs):
            out_ref[...] = mine(r)
        return
    early, w_ref, out_refs = refs[:near], refs[near], refs[near + 1 :]
    w_mine = reordered(w_ref[...], me_ref[1], order).astype(BF16)
    rank = w_mine.shape[1]
    for r, out_ref in enumerate(out_refs):
        if r < near:
            before = early[r].shape[0]
            out_ref[:before, :pixels] = early[r][...]
            out_ref[before:, :pixels] = mine(r)
            out_ref[:, pixels:] = w_mine
        else:
            out_ref[:, :pixels] = mine(r)
            for i in range(w_mine.shape[0] // frames):
                out_ref[:, pixels + rank * i : pixels + rank * (i + 1)] = w_mine[frames * i : frames * (i + 1)]


def correct(raw_frames, gain_map, coupling, at, parts, start, count, early=None, factor_w=None, order=None):
    frames, rows, cols = raw_frames.shape
    group = 16
    pixels = rows * cols // parts
    first = start // group
    if early is None:
        extra, near = [], None
        shapes = [(count, pixels)] * parts
        out_specs = [pl.BlockSpec((group, pixels), lambda i, m: (i, 0))] * parts
    else:
        rank = factor_w.shape[1]
        extra, near = [*early, factor_w], len(early)
        shapes = [(frames, pixels + rank)] * near + [(group, pixels + rank * (frames // group))] * (parts - near)
        out_specs = [pl.BlockSpec(shape, lambda i, m: (0, 0)) for shape in shapes]
    return pl.pallas_call(
        functools.partial(stencil_body, start=start, order=order, near=near),
        out_shape=[jax.ShapeDtypeStruct(shape, BF16) for shape in shapes],
        grid_spec=pltpu.PrefetchScalarGridSpec(
            num_scalar_prefetch=1,
            grid=(count // group,),
            in_specs=[
                pl.BlockSpec((group * rows, cols), lambda i, m: (i + first, 0)),
                pl.BlockSpec((rows, cols), lambda i, m: (0, 0)),
                pl.BlockSpec((rows, cols), lambda i, m: (0, 0)),
            ]
            + [pl.BlockSpec(x.shape, lambda i, m: (0, 0)) for x in extra],
            out_specs=out_specs,
            scratch_shapes=[pltpu.VMEM((rows, cols), F32)] * 2 + [pltpu.VMEM((parts, group, pixels), BF16)],
        ),
        cost_estimate=pl.CostEstimate(
            flops=count * rows * cols * SWEEPS * 9,
            bytes_accessed=count * rows * cols * 6,
            transcendentals=0,
        ),
        name="charge_sharing",
    )(at, raw_frames.reshape(frames * rows, cols), gain_map, coupling, *extra)


TILE = 256
PARTS = 2


def ratio_tile(data_refs, w, h_refs, at, tile):
    h_tile = jnp.concatenate([ref[:, at : at + tile] for ref in h_refs], axis=0)
    product = jnp.dot(w, h_tile, preferred_element_type=F32)
    values = jnp.concatenate([ref[:, at : at + tile] for ref in data_refs], axis=0).astype(F32)
    return (values / product).astype(BF16), h_tile


def w_term_body(*refs):
    *data_refs, h_one, h_two, out_ref = refs
    pixels = h_one.shape[1]
    rank = out_ref.shape[1]
    w = jnp.concatenate([ref[:, at : at + rank] for ref in data_refs for at in range(pixels, ref.shape[1], rank)], axis=0)
    tile = min(TILE, pixels)
    ones = jnp.ones((16, tile), BF16)
    total = None
    for at in range(0, pixels, tile):
        ratio, h_tile = ratio_tile(data_refs, w, (h_one, h_two), at, tile)
        ratio = jnp.concatenate([ratio, ones], axis=0)
        term = lax.dot_general(ratio, h_tile, (((1,), (1,)), ((), ())), preferred_element_type=F32)
        total = term if total is None else total + term
    out_ref[...] = total


def tiles_body(*refs):
    *data_refs, out_ref = refs
    pixels = out_ref.shape[1]
    row = 0
    for ref in data_refs:
        out_ref[row : row + ref.shape[0], :] = ref[:, :pixels]
        row += ref.shape[0]


VMEM = pl.BlockSpec(memory_space=pltpu.VMEM)


def term(body, shape, dtype, args, flops):
    return pl.pallas_call(
        body,
        out_shape=pltpu.VMEM(shape, dtype),
        in_specs=[VMEM] * len(args),
        out_specs=VMEM,
        cost_estimate=pl.CostEstimate(flops=flops, bytes_accessed=sum(a.size * 2 for a in args), transcendentals=0),
        compiler_params=pltpu.CompilerParams(vmem_limit_bytes=8 << 20),
    )(*[pltpu.with_memory_space_constraint(a, pltpu.VMEM) for a in args])


def halves(value):
    high = value.astype(F16)
    return high, (value - high.astype(F32)).astype(F16)


def with_sums(block, sums):
    high, low = halves(sums)
    return jnp.concatenate([block.astype(F16), high[None], low[None], jnp.zeros((14, len(sums)), F16)], axis=0)


def groups_of(n_pix):
    return [list(range(n_pix // 2)), list(range(n_pix - 1, n_pix // 2 - 1, -1))]


def local(raw_frames, gain_map, coupling, factor_w, factor_h, n_scan, n_pix):
    scan_bits = n_scan.bit_length() - 1
    scan = lax.axis_index("scan")
    me = lax.axis_index("pix")
    row_count, rank = factor_w.shape
    comp_rows, pixels = factor_h.shape
    half = rank // 2
    x_bits = [1 << b for b in range(1, scan_bits)]
    far = list(range(2, n_pix, 2))
    even = [0] + far
    odd = [r + 1 for r in even]
    scale = 1.0 / (pixels // 8)

    def over_pix(value, bit):
        return lax.ppermute(value, "pix", [(i, i ^ bit) for i in range(n_pix)])

    def over_scan(value, bit):
        return lax.ppermute(value, "scan", [(i, i ^ bit) for i in range(n_scan)])

    comp_order = [2 * j + c for c in range(2) for j in range(n_scan // 2)]
    back_order = [comp_order.index(j) for j in range(n_scan)]

    def to_global(w):
        at = [w[:, comp_rows * i : comp_rows * (i + 1)] for i in back_order]
        return jnp.concatenate(relative(at, scan), axis=1)

    w_local = reordered(factor_w, scan, comp_order)

    close = n_pix // 2
    frames = raw_frames.shape[0]
    tile = {r: [] for r in range(n_pix)}
    at = jnp.stack([me, scan]).astype(jnp.int32)
    early = correct(raw_frames, gain_map, coupling, at, n_pix, 0, frames - 16)
    late = correct(raw_frames, gain_map, coupling, at, n_pix, frames - 16, 16, early[:close], factor_w, comp_order)
    for c, messages in enumerate([early, late]):
        for r in range(1, n_pix):
            if c or r >= close:
                tile[r].append(over_pix(messages[r], r))
    tile[0].append(late[0])

    for bit in x_bits:
        factor_h = jnp.concatenate([factor_h, over_scan(factor_h, bit)], 0)
    width = pixels // PARTS
    parts = [slice(width * c, width * (c + 1)) for c in range(PARTS)]
    h_mine = factor_h.astype(BF16)
    h_other = over_scan(h_mine, 1)
    h_own = [factor_h[:, part] for part in parts]
    h_pairs = [[h_mine[:, part], h_other[:, part]] for part in parts]

    def blocks(which):
        return [part for r in which for part in tile[r]]

    for rounds in range(ITERS):
        if rounds:
            h_part = sum(jnp.concatenate([jnp.sum(h.astype(F32), axis=1) for h in pair]) for pair in h_pairs)

        def ratio_of(values, w_round, pair):
            product = jnp.dot(w_round, jnp.concatenate(pair, axis=0), preferred_element_type=F32)
            return (values.astype(F32) / product).astype(BF16)

        def numerator_of(values, w_round):
            terms = []
            for part, pair in zip(parts, h_pairs):
                ratio = ratio_of(values[:, part], w_round, pair)
                h_block = jnp.concatenate(pair, axis=0)
                terms.append(lax.dot_general(ratio, h_block, (((1,), (1,)), ((), ())), preferred_element_type=F32))
            return sum(terms)

        if rounds == 0:
            backs, h_here = [], [h_mine, h_other]
            for group in groups_of(n_pix):
                rows = row_count * len(group)
                shape = (rows + 16, rank)
                partial = term(w_term_body, shape, F32, blocks(group) + h_here, 4 * rows * rank * pixels) * scale
                h_sums = partial[rows]
                messages = {}
                for j, r in enumerate(group):
                    block = partial[row_count * j : row_count * (j + 1)]
                    if r == 0:
                        numerator = block
                    else:
                        messages[r] = with_sums(block, h_sums)
                h_here, messages = lax.optimization_barrier((h_here, messages))
                for r, message in messages.items():
                    backs.append(over_pix(message, r))
            everything = functools.reduce(lambda a, b: a + b, [b.astype(F32) for b in backs])
            numerator = numerator + everything[:row_count]
            h_sums = h_sums + everything[row_count] + everything[row_count + 1]
        else:
            rows = row_count * len(even)
            away = numerator_of(data_odd, w_odd)
            back = over_pix(with_sums(away / h_part - 1.0, h_part), 1)
            near = lax.optimization_barrier(numerator_of(data_even, w_even))
            weight = back[rows].astype(F32) + back[rows + 1].astype(F32)
            near = near + (back[:rows].astype(F32) + 1.0) * weight
            h_two = h_part + weight
            numerator, h_sums = near[:row_count], h_two
            for i, r in enumerate(far):
                mean = near[row_count * (i + 1) : row_count * (i + 2)] / h_two - 1.0
                back = over_pix(with_sums(mean, h_two), r)
                weight = back[row_count].astype(F32) + back[row_count + 1].astype(F32)
                numerator = numerator + (back[:row_count].astype(F32) + 1.0) * weight
                h_sums = h_sums + weight
        w_local = w_local * numerator / h_sums

        w_mine = w_local.astype(BF16)
        w_even = jnp.concatenate([w_mine] + [over_pix(w_mine, r) for r in far], axis=0)
        w_odd = over_pix(w_even, 1)
        if rounds == 0:
            shape = (row_count * len(even), pixels)
            data_even = term(tiles_body, shape, BF16, blocks(even), 0)
            data_odd = term(tiles_body, shape, BF16, blocks(odd), 0)

        def numerator_rows(w, ratio):
            return lax.dot_general(w, ratio, (((0,), (0,)), ((), ())), preferred_element_type=F32)

        last = rounds == ITERS - 1
        w_part = jnp.sum(w_even.astype(F32), axis=0) + jnp.sum(w_odd.astype(F32), axis=0)
        w_sums = w_part[:half] + over_scan(w_part[half:], 1)
        evens = []
        for part, pair in zip(parts, h_pairs):
            ratio = ratio_of(data_even[:, part], w_even, pair)
            evens.append([numerator_rows(w, ratio) for w in (w_even[:, :half], w_even[:, half:])])
        totals = []
        for c, (part, pair) in enumerate(zip(parts, h_pairs)):
            ratio = ratio_of(data_odd[:, part], w_odd, pair)
            other = over_scan(evens[c][1] + numerator_rows(w_odd[:, half:], ratio), 1)
            totals.append(evens[c][0] + numerator_rows(w_odd[:, :half], ratio) + other)
        for bit in x_bits[::-1]:
            count = totals[0].shape[0] // comp_rows
            step = bit >> 1
            if last:
                keep = [i for i in range(count) if not i & step]
                send = [i | step for i in keep]
            else:
                keep = list(range(count))
                send = [i ^ step for i in keep]

            def pick(value, which):
                if list(which) == list(range(which[0], which[0] + len(which))):
                    return value[comp_rows * which[0] : comp_rows * (which[-1] + 1)]
                return jnp.concatenate([value[comp_rows * i : comp_rows * (i + 1)] for i in which], axis=0)

            sums = pick(w_sums, send)
            weight = over_scan(sums, bit)
            for c in range(PARTS):
                message = (pick(totals[c], send) / sums[:, None] - 1.0).astype(F16)
                back = over_scan(message, bit).astype(F32) + 1.0
                totals[c] = pick(totals[c], keep) + back * weight[:, None]
            w_sums = pick(w_sums, keep) + weight
        for c in range(PARTS):
            h_own[c] = h_own[c][: totals[c].shape[0]] * totals[c] / w_sums[:, None]
            if not last:
                h_mine = h_own[c].astype(BF16)
                h_pairs[c] = [h_mine, over_scan(h_mine, 1)]
    return (to_global(w_local), jnp.concatenate(h_own, axis=1))


def solution(mesh):
    n_pix = mesh.shape["pix"]

    def layer(*args):
        return local(*args, n_scan=mesh.shape["scan"], n_pix=n_pix)

    return jax.shard_map(
        layer,
        mesh=mesh,
        in_specs=(
            P(("scan", "pix"), None, None),
            P(),
            P(),
            P(("scan", "pix"), None),
            P("scan", "pix"),
        ),
        out_specs=(P(("scan", "pix"), None), P("scan", "pix")),
        check_vma=False,
    )
```

```python
import functools

import jax
import jax.numpy as jnp
from jax import lax
from jax.experimental import pallas as pl
from jax.experimental.pallas import tpu as pltpu
from jax.sharding import PartitionSpec as P

SWEEPS = 4
ITERS = 2
BF16, F16, F32 = jnp.bfloat16, jnp.float16, jnp.float32


def relative(blocks, index):
    for bit in range(len(blocks).bit_length() - 1):
        flip = (index >> bit) & 1
        blocks = [jnp.where(flip == 1, blocks[j ^ (1 << bit)], blocks[j]) for j in range(len(blocks))]
    return blocks


def reordered(w, index, order):
    width = w.shape[1] // len(order)
    blocks = relative([w[:, width * j : width * (j + 1)] for j in range(len(order))], index)
    return jnp.concatenate([blocks[j] for j in order], axis=1)


def stencil_body(me_ref, raw_ref, gain_ref, couple_ref, *refs, start, order, near):
    refs, (gain_s, near_s, stage) = refs[:-3], refs[-3:]
    rows, cols = gain_ref.shape
    parts, frames, pixels = stage.shape
    groups = frames // 8
    band = rows // parts

    @pl.when(pl.program_id(0) == 0)
    def _():
        inverse = 1.0 / (1.0 + 4.0 * couple_ref[...])
        gain_s[...] = gain_ref[...] * inverse
        near_s[...] = couple_ref[...] * inverse

    lane = lax.broadcasted_iota(jnp.int32, (8, cols), 1)
    has_left = jnp.where(lane == 0, 0.0, 1.0)
    has_right = jnp.where(lane == cols - 1, 0.0, 1.0)
    zero = jnp.zeros((8, cols), F32)

    def every(ref, row):
        return ref[pl.ds(row, 8, stride=0), :]

    def advance(state, row, end=False):
        levels, scaled, weight = state
        if end:
            w_new = zero
            enter = [zero] * groups
            s_new = [zero] * groups
        else:
            w_new = every(near_s, row)
            gain = every(gain_ref, row)
            gain_scaled = every(gain_s, row)
            raws = [raw_ref[pl.ds(g * 8 * rows + row, 8, stride=rows), :] for g in range(groups)]
            enter = [raw * gain for raw in raws]
            s_new = [raw * gain_scaled for raw in raws]
        out, new_levels = [], []
        for g in range(groups):
            new = enter[g]
            mine = []
            for k in range(SWEEPS):
                older, newer = levels[g][k]
                side = pltpu.roll(newer, 1, 1) * has_left + pltpu.roll(newer, cols - 1, 1) * has_right
                value = scaled[g][k] + weight[k] * ((older + side) + new)
                mine.append((newer, new))
                new = value
            out.append(new)
            new_levels.append(mine)
        scaled = [[s_new[g]] + scaled[g][: SWEEPS - 1] for g in range(groups)]
        return (new_levels, scaled, [w_new] + weight[: SWEEPS - 1]), out

    frame = lax.broadcasted_iota(jnp.int32, (frames, cols), 0) + frames * pl.program_id(0) + start
    phase = frame.astype(F32) * 0.6180340 + lax.broadcasted_iota(jnp.int32, (frames, cols), 1).astype(F32) * 0.7548777
    shift = (phase - jnp.floor(phase) - 0.5) * 0.005

    def one_band(part, state, error, first=False, last=False):
        for i in range(band):
            state, out = advance(state, part * band + SWEEPS + i, end=last and i + SWEEPS >= band)
            value = jnp.concatenate(out, axis=0)
            value = value + (value * shift if first and i == 0 else error)
            rounded = value.astype(BF16)
            error = value - rounded.astype(F32)
            stage[part, :, i * cols : (i + 1) * cols] = rounded
        return state, error

    state = (
        [[(zero, zero)] * SWEEPS for _ in range(groups)],
        [[zero] * SWEEPS for _ in range(groups)],
        [zero] * SWEEPS,
    )
    for row in range(SWEEPS):
        state, _ = advance(state, row)
    carry = one_band(0, state, None, first=True)
    carry = lax.fori_loop(1, parts - 1, lambda part, c: one_band(part, *c), carry)
    one_band(parts - 1, *carry, last=True)

    def mine(r):
        return stage[jnp.bitwise_xor(me_ref[0], r)]

    if near is None:
        for r, out_ref in enumerate(refs):
            out_ref[...] = mine(r)
        return
    early, w_ref, out_refs = refs[:near], refs[near], refs[near + 1 :]
    w_mine = reordered(w_ref[...], me_ref[1], order).astype(BF16)
    rank = w_mine.shape[1]
    for r, out_ref in enumerate(out_refs):
        if r < near:
            before = early[r].shape[0]
            out_ref[:before, :pixels] = early[r][...]
            out_ref[before:, :pixels] = mine(r)
            out_ref[:, pixels:] = w_mine
        else:
            out_ref[:, :pixels] = mine(r)
            for i in range(w_mine.shape[0] // frames):
                out_ref[:, pixels + rank * i : pixels + rank * (i + 1)] = w_mine[frames * i : frames * (i + 1)]


def correct(raw_frames, gain_map, coupling, at, parts, start, count, early=None, factor_w=None, order=None):
    frames, rows, cols = raw_frames.shape
    group = 16
    pixels = rows * cols // parts
    first = start // group
    if early is None:
        extra, near = [], None
        shapes = [(count, pixels)] * parts
        out_specs = [pl.BlockSpec((group, pixels), lambda i, m: (i, 0))] * parts
    else:
        rank = factor_w.shape[1]
        extra, near = [*early, factor_w], len(early)
        shapes = [(frames, pixels + rank)] * near + [(group, pixels + rank * (frames // group))] * (parts - near)
        out_specs = [pl.BlockSpec(shape, lambda i, m: (0, 0)) for shape in shapes]
    return pl.pallas_call(
        functools.partial(stencil_body, start=start, order=order, near=near),
        out_shape=[jax.ShapeDtypeStruct(shape, BF16) for shape in shapes],
        grid_spec=pltpu.PrefetchScalarGridSpec(
            num_scalar_prefetch=1,
            grid=(count // group,),
            in_specs=[
                pl.BlockSpec((group * rows, cols), lambda i, m: (i + first, 0)),
                pl.BlockSpec((rows, cols), lambda i, m: (0, 0)),
                pl.BlockSpec((rows, cols), lambda i, m: (0, 0)),
            ]
            + [pl.BlockSpec(x.shape, lambda i, m: (0, 0)) for x in extra],
            out_specs=out_specs,
            scratch_shapes=[pltpu.VMEM((rows, cols), F32)] * 2 + [pltpu.VMEM((parts, group, pixels), BF16)],
        ),
        cost_estimate=pl.CostEstimate(
            flops=count * rows * cols * SWEEPS * 9,
            bytes_accessed=count * rows * cols * 6,
            transcendentals=0,
        ),
        name="charge_sharing",
    )(at, raw_frames.reshape(frames * rows, cols), gain_map, coupling, *extra)


TILE = 256
PARTS = 2


def w_term_body(*refs, count, carried, scale):
    out_ref = refs[-1]
    data_refs, rest = refs[:count], list(refs[count:-1])
    rank = out_ref.shape[1]
    rows = sum(ref.shape[0] for ref in data_refs)
    by = None if carried else rest.pop(0)[...]
    w_ref = None if carried else rest.pop(0)
    pixels = sum(ref.shape[1] for ref in rest[::2])
    if carried:
        w = jnp.concatenate([ref[:, at : at + rank] for ref in data_refs for at in range(pixels, ref.shape[1], rank)], axis=0)
    else:
        w = w_ref[...]
    total, start = None, 0
    for pair in zip(rest[::2], rest[1::2]):
        width = pair[0].shape[1]
        tile = min(TILE, width)
        ones = jnp.ones((16, tile), BF16)
        for at in range(0, width, tile):
            h_tile = jnp.concatenate([ref[:, at : at + tile] for ref in pair], axis=0)
            product = jnp.dot(w, h_tile, preferred_element_type=F32)
            values = jnp.concatenate([ref[:, start + at : start + at + tile] for ref in data_refs], axis=0).astype(F32)
            ratio = jnp.concatenate([(values / product).astype(BF16), ones], axis=0)
            term = lax.dot_general(ratio, h_tile, (((1,), (1,)), ((), ())), preferred_element_type=F32)
            total = term if total is None else total + term
        start += width
    sums = total[rows : rows + 1]
    if carried:
        numerators, sums = total[:rows] * scale, sums * scale
    else:
        numerators, sums = (total[:rows] - sums) / by, sums / by
    high = sums.astype(BF16).astype(F32)
    line = lax.broadcasted_iota(jnp.int32, (16, rank), 0)
    out_ref[:rows] = numerators
    out_ref[rows:] = jnp.where(line == 0, high, jnp.where(line == 1, sums - high, 0.0))


def tiles_body(*refs):
    *data_refs, out_ref = refs
    pixels = out_ref.shape[1]
    row = 0
    for ref in data_refs:
        out_ref[row : row + ref.shape[0], :] = ref[:, :pixels]
        row += ref.shape[0]


VMEM = pl.BlockSpec(memory_space=pltpu.VMEM)


def term(body, shape, dtype, args, flops):
    return pl.pallas_call(
        body,
        out_shape=pltpu.VMEM(shape, dtype),
        in_specs=[VMEM] * len(args),
        out_specs=VMEM,
        cost_estimate=pl.CostEstimate(flops=flops, bytes_accessed=sum(a.size * 2 for a in args), transcendentals=0),
        compiler_params=pltpu.CompilerParams(vmem_limit_bytes=8 << 20),
    )(*[pltpu.with_memory_space_constraint(a, pltpu.VMEM) for a in args])


def groups_of(n_pix):
    far = list(range(n_pix - 1, n_pix // 2 - 1, -1))
    return [list(range(n_pix // 2)), far[: len(far) // 2], far[len(far) // 2 :]]


def local(raw_frames, gain_map, coupling, factor_w, factor_h, n_scan, n_pix):
    scan_bits = n_scan.bit_length() - 1
    scan = lax.axis_index("scan")
    me = lax.axis_index("pix")
    row_count, rank = factor_w.shape
    comp_rows, pixels = factor_h.shape
    half = rank // 2
    x_bits = [1 << b for b in range(1, scan_bits)]
    far = list(range(2, n_pix, 2))
    even = [0] + far
    odd = [r + 1 for r in even]
    scale = 1.0 / (pixels // 8)

    def over_pix(value, bit):
        return lax.ppermute(value, "pix", [(i, i ^ bit) for i in range(n_pix)])

    def over_scan(value, bit):
        return lax.ppermute(value, "scan", [(i, i ^ bit) for i in range(n_scan)])

    comp_order = [2 * j + c for c in range(2) for j in range(n_scan // 2)]
    back_order = [comp_order.index(j) for j in range(n_scan)]

    def to_global(w):
        at = [w[:, comp_rows * i : comp_rows * (i + 1)] for i in back_order]
        return jnp.concatenate(relative(at, scan), axis=1)

    w_local = reordered(factor_w, scan, comp_order)

    close = n_pix // 2
    frames = raw_frames.shape[0]
    tile = {r: [] for r in range(n_pix)}
    at = jnp.stack([me, scan]).astype(jnp.int32)
    early = correct(raw_frames, gain_map, coupling, at, n_pix, 0, frames - 16)
    late = correct(raw_frames, gain_map, coupling, at, n_pix, frames - 16, 16, early[:close], factor_w, comp_order)
    for c, messages in enumerate([early, late]):
        for r in range(1, n_pix):
            if c or r >= close:
                tile[r].append(over_pix(messages[r], r))
    tile[0].append(late[0])

    for bit in x_bits:
        factor_h = jnp.concatenate([factor_h, over_scan(factor_h, bit)], 0)
    width = pixels // PARTS
    parts = [slice(width * c, width * (c + 1)) for c in range(PARTS)]
    h_mine = factor_h.astype(BF16)
    h_other = over_scan(h_mine, 1)
    h_own = [factor_h[:, part] for part in parts]
    h_pairs = [[h_mine[:, part], h_other[:, part]] for part in parts]

    def blocks(which):
        return [part for r in which for part in tile[r]]

    for rounds in range(ITERS):
        def ratio_of(values, w_round, pair):
            product = jnp.dot(w_round, jnp.concatenate(pair, axis=0), preferred_element_type=F32)
            return (values.astype(F32) / product).astype(BF16)

        def w_term(data, h_list, w=None):
            rows = sum(d.shape[0] for d in data)
            body = functools.partial(w_term_body, count=len(data), carried=w is None, scale=scale)
            args = [*data, *([] if w is None else [first_sums, w]), *h_list]
            return term(body, (rows + 16, rank), F32, args, 4 * rows * rank * pixels)

        def block_of(values, i):
            rows = values.shape[0] - 16
            return jnp.concatenate([values[row_count * i : row_count * (i + 1)], values[rows:]], axis=0)

        def combined(values, others):
            return functools.reduce(lambda a, b: a + b, [o.astype(F32) for o in others], values)

        if rounds == 0:
            backs, h_here = [], [h_mine, h_other]
            for group in groups_of(n_pix):
                partial = w_term(blocks(group), h_here)
                messages = {}
                for j, r in enumerate(group):
                    if r == 0:
                        numerator = block_of(partial, j)
                    else:
                        messages[r] = block_of(partial, j).astype(F16)
                h_here, messages = lax.optimization_barrier((h_here, messages))
                for r, message in messages.items():
                    backs.append(over_pix(message, r))
            numerator = combined(numerator, backs)
            h_sums = numerator[row_count : row_count + 1] + numerator[row_count + 1 : row_count + 2]
            first_sums = h_sums
            w_local = w_local * numerator[:row_count] / h_sums
        else:
            h_list = [h for pair in h_pairs for h in pair]
            back = over_pix(w_term([data_odd], h_list, w_odd).astype(F16), 1)
            near = w_term([data_even], h_list, w_even)
            near = combined(near, [back])
            backs = [over_pix(block_of(near, i + 1).astype(F16), r) for i, r in enumerate(far)]
            numerator = combined(block_of(near, 0), backs)
            h_sums = numerator[row_count : row_count + 1] + numerator[row_count + 1 : row_count + 2]
            w_local = w_local * (numerator[:row_count] + h_sums) / h_sums

        w_mine = w_local.astype(BF16)
        w_even = jnp.concatenate([w_mine] + [over_pix(w_mine, r) for r in far], axis=0)
        w_odd = over_pix(w_even, 1)
        if rounds == 0:
            shape = (row_count * len(even), pixels)
            data_even = term(tiles_body, shape, BF16, blocks(even), 0)
            data_odd = term(tiles_body, shape, BF16, blocks(odd), 0)

        def numerator_rows(w, ratio):
            return lax.dot_general(w, ratio, (((0,), (0,)), ((), ())), preferred_element_type=F32)

        last = rounds == ITERS - 1
        w_part = jnp.sum(w_even.astype(F32), axis=0) + jnp.sum(w_odd.astype(F32), axis=0)
        w_sums = w_part[:half] + over_scan(w_part[half:], 1)
        evens = []
        for part, pair in zip(parts, h_pairs):
            ratio = ratio_of(data_even[:, part], w_even, pair)
            evens.append([numerator_rows(w, ratio) for w in (w_even[:, :half], w_even[:, half:])])
        totals = []
        for c, (part, pair) in enumerate(zip(parts, h_pairs)):
            w_here = w_odd
            if c:
                w_here, _ = lax.optimization_barrier((w_odd, other))
            ratio = ratio_of(data_odd[:, part], w_here, pair)
            other = evens[c][1] + numerator_rows(w_here[:, half:], ratio)
            totals.append(evens[c][0] + numerator_rows(w_here[:, :half], ratio) + over_scan(other, 1))
        for bit in x_bits[::-1]:
            count = totals[0].shape[0] // comp_rows
            step = bit >> 1
            if last:
                keep = [i for i in range(count) if not i & step]
                send = [i | step for i in keep]
            else:
                keep = list(range(count))
                send = [i ^ step for i in keep]

            def pick(value, which):
                if list(which) == list(range(which[0], which[0] + len(which))):
                    return value[comp_rows * which[0] : comp_rows * (which[-1] + 1)]
                return jnp.concatenate([value[comp_rows * i : comp_rows * (i + 1)] for i in which], axis=0)

            sums = pick(w_sums, send)
            weight = over_scan(sums, bit)
            backs = []
            for c in range(PARTS):
                value = totals[c]
                if c:
                    value, _ = lax.optimization_barrier((value, message))
                message = (pick(value, send) / sums[:, None] - 1.0).astype(F16)
                backs.append(over_scan(message, bit))
            for c in range(PARTS):
                if c and bit == x_bits[0]:
                    backs[c], h_own[c - 1] = lax.optimization_barrier((backs[c], h_own[c - 1]))
                totals[c] = pick(totals[c], keep) + (backs[c].astype(F32) + 1.0) * weight[:, None]
                if bit == x_bits[0]:
                    h_own[c] = h_own[c][: totals[c].shape[0]] * totals[c] / (pick(w_sums, keep) + weight)[:, None]
                    if not last:
                        h_mine = h_own[c].astype(BF16)
                        h_pairs[c] = [h_mine, over_scan(h_mine, 1)]
            w_sums = pick(w_sums, keep) + weight
    return (to_global(w_local), jnp.concatenate(h_own, axis=1))


def solution(mesh):
    n_pix = mesh.shape["pix"]

    def layer(*args):
        return local(*args, n_scan=mesh.shape["scan"], n_pix=n_pix)

    return jax.shard_map(
        layer,
        mesh=mesh,
        in_specs=(
            P(("scan", "pix"), None, None),
            P(),
            P(),
            P(("scan", "pix"), None),
            P("scan", "pix"),
        ),
        out_specs=(P(("scan", "pix"), None), P("scan", "pix")),
        check_vma=False,
    )
```

```python
import functools

import jax
import jax.numpy as jnp
from jax import lax
from jax.experimental import pallas as pl
from jax.experimental.pallas import tpu as pltpu
from jax.sharding import PartitionSpec as P

SWEEPS = 4
ITERS = 2
BF16, F16, F32 = jnp.bfloat16, jnp.float16, jnp.float32


def relative(blocks, index):
    for bit in range(len(blocks).bit_length() - 1):
        flip = (index >> bit) & 1
        blocks = [jnp.where(flip == 1, blocks[j ^ (1 << bit)], blocks[j]) for j in range(len(blocks))]
    return blocks


def reordered(w, index, order):
    width = w.shape[1] // len(order)
    blocks = relative([w[:, width * j : width * (j + 1)] for j in range(len(order))], index)
    return jnp.concatenate([blocks[j] for j in order], axis=1)


def stencil_body(raw_ref, gain_ref, couple_ref, *refs, start, order, far):
    refs, (gain_s, near_s, stage) = refs[:-3], refs[-3:]
    rows, cols = gain_ref.shape
    parts, frames, pixels = stage.shape
    groups = frames // 8
    band = rows // (2 * parts)
    me = lax.axis_index("pix")
    own_half = me // parts
    half = 1 - own_half if far else own_half
    first_row = half * (rows // 2)
    above = half.astype(F32)
    below = 1.0 - above

    @pl.when(pl.program_id(0) == 0)
    def _():
        inverse = 1.0 / (1.0 + 4.0 * couple_ref[...])
        gain_s[...] = gain_ref[...] * inverse
        near_s[...] = couple_ref[...] * inverse

    lane = lax.broadcasted_iota(jnp.int32, (8, cols), 1)
    has_left = jnp.where(lane == 0, 0.0, 1.0)
    has_right = jnp.where(lane == cols - 1, 0.0, 1.0)
    zero = jnp.zeros((8, cols), F32)

    def every(ref, row):
        return ref[pl.ds(row, 8, stride=0), :]

    def advance(state, row, there=None):
        levels, scaled, weight = state
        w_new = every(near_s, row)
        gain = every(gain_ref, row)
        gain_scaled = every(gain_s, row)
        if there is not None:
            w_new, gain, gain_scaled = w_new * there, gain * there, gain_scaled * there
        raws = [raw_ref[pl.ds(g * 8 * rows + row, 8, stride=rows), :] for g in range(groups)]
        enter = [raw * gain for raw in raws]
        s_new = [raw * gain_scaled for raw in raws]
        out, new_levels = [], []
        for g in range(groups):
            new = enter[g]
            mine = []
            for k in range(SWEEPS):
                older, newer = levels[g][k]
                side = pltpu.roll(newer, 1, 1) * has_left + pltpu.roll(newer, cols - 1, 1) * has_right
                value = scaled[g][k] + weight[k] * ((older + side) + new)
                mine.append((newer, new))
                new = value
            out.append(new)
            new_levels.append(mine)
        scaled = [[s_new[g]] + scaled[g][: SWEEPS - 1] for g in range(groups)]
        return (new_levels, scaled, [w_new] + weight[: SWEEPS - 1]), out

    frame = lax.broadcasted_iota(jnp.int32, (frames, cols), 0) + frames * pl.program_id(0) + start
    phase = frame.astype(F32) * 0.6180340 + lax.broadcasted_iota(jnp.int32, (frames, cols), 1).astype(F32) * 0.7548777
    shift = (phase - jnp.floor(phase) - 0.5) * 0.005

    def one_band(part, state, error, first=False, last=False):
        for i in range(band):
            if last and i + SWEEPS >= band:
                row = jnp.minimum(first_row + rows // 2 + (i + SWEEPS - band), rows - 1)
                state, out = advance(state, row, below)
            else:
                state, out = advance(state, first_row + part * band + SWEEPS + i)
            value = jnp.concatenate(out, axis=0)
            value = value + (value * shift if first and i == 0 else error)
            rounded = value.astype(BF16)
            error = value - rounded.astype(F32)
            stage[part, :, i * cols : (i + 1) * cols] = rounded
        return state, error

    state = (
        [[(zero, zero)] * SWEEPS for _ in range(groups)],
        [[zero] * SWEEPS for _ in range(groups)],
        [zero] * SWEEPS,
    )
    for i in range(SWEEPS):
        state, _ = advance(state, jnp.maximum(first_row - SWEEPS + i, 0), above)
    for i in range(SWEEPS):
        state, _ = advance(state, first_row + i)
    carry = one_band(0, state, None, first=True)
    carry = lax.fori_loop(1, parts - 1, lambda part, c: one_band(part, *c), carry)
    one_band(parts - 1, *carry, last=True)
    w = None
    if order is not None:
        w, refs = reordered(refs[0][...], lax.axis_index("scan"), order).astype(BF16), refs[1:]
    for r, out_ref in enumerate(refs):
        out_ref[:, :pixels] = stage[jnp.bitwise_xor(me, r) % parts]
        for i in range(0 if w is None else w.shape[0] // frames):
            at, rank = pixels + w.shape[1] * i, w.shape[1]
            out_ref[:, at : at + rank] = w[frames * i : frames * (i + 1)]


def correct(raw_frames, gain_map, coupling, parts, far, start, count, factor_w=None, order=None):
    frames, rows, cols = raw_frames.shape
    group = 16
    pixels = rows * cols // parts
    first = start // group
    extra, specs, width = [], [], pixels
    if factor_w is not None:
        rank = factor_w.shape[1]
        extra = [factor_w]
        if count == frames:
            specs, width = [pl.BlockSpec((group, rank), lambda i: (i, 0))], pixels + rank
        else:
            specs, width = [pl.BlockSpec((frames, rank), lambda i: (0, 0))], pixels + rank * (frames // group)
    return pl.pallas_call(
        functools.partial(stencil_body, start=start, order=order, far=far),
        out_shape=[jax.ShapeDtypeStruct((count, width), BF16)] * (parts // 2),
        grid_spec=pl.GridSpec(
            grid=(count // group,),
            in_specs=[
                pl.BlockSpec((group * rows, cols), lambda i: (i + first, 0)),
                pl.BlockSpec((rows, cols), lambda i: (0, 0)),
                pl.BlockSpec((rows, cols), lambda i: (0, 0)),
            ]
            + specs,
            out_specs=[pl.BlockSpec((group, width), lambda i: (i, 0))] * (parts // 2),
            scratch_shapes=[pltpu.VMEM((rows, cols), F32)] * 2 + [pltpu.VMEM((parts // 2, group, pixels), BF16)],
        ),
        cost_estimate=pl.CostEstimate(
            flops=count * rows * cols * SWEEPS * 5,
            bytes_accessed=count * rows * cols * 5,
            transcendentals=0,
        ),
        name="charge_sharing",
    )(raw_frames.reshape(frames * rows, cols), gain_map, coupling, *extra)


TILE = 256
PARTS = 2


def w_term_body(*refs, count, carried, scale):
    out_ref = refs[-1]
    data_refs, rest = refs[:count], list(refs[count:-1])
    rank = out_ref.shape[1]
    rows = sum(ref.shape[0] for ref in data_refs)
    by = None if carried else rest.pop(0)[...]
    w_ref = None if carried else rest.pop(0)
    pixels = sum(ref.shape[1] for ref in rest[::2])
    if carried:
        w = jnp.concatenate([ref[:, at : at + rank] for ref in data_refs for at in range(pixels, ref.shape[1], rank)], axis=0)
    else:
        w = w_ref[...]
    total, start = None, 0
    for pair in zip(rest[::2], rest[1::2]):
        width = pair[0].shape[1]
        tile = min(TILE, width)
        ones = jnp.ones((16, tile), BF16)
        for at in range(0, width, tile):
            h_tile = jnp.concatenate([ref[:, at : at + tile] for ref in pair], axis=0)
            product = jnp.dot(w, h_tile, preferred_element_type=F32)
            values = jnp.concatenate([ref[:, start + at : start + at + tile] for ref in data_refs], axis=0).astype(F32)
            ratio = jnp.concatenate([(values / product).astype(BF16), ones], axis=0)
            term = lax.dot_general(ratio, h_tile, (((1,), (1,)), ((), ())), preferred_element_type=F32)
            total = term if total is None else total + term
        start += width
    sums = total[rows : rows + 1]
    if carried:
        numerators, sums = total[:rows] * scale, sums * scale
    else:
        numerators, sums = (total[:rows] - sums) / by, sums / by
    high = sums.astype(BF16).astype(F32)
    line = lax.broadcasted_iota(jnp.int32, (16, rank), 0)
    out_ref[:rows] = numerators
    out_ref[rows:] = jnp.where(line == 0, high, jnp.where(line == 1, sums - high, 0.0))


def tiles_body(*refs):
    *data_refs, out_ref = refs
    pixels = out_ref.shape[1]
    row = 0
    for ref in data_refs:
        out_ref[row : row + ref.shape[0], :] = ref[:, :pixels]
        row += ref.shape[0]


VMEM = pl.BlockSpec(memory_space=pltpu.VMEM)


def term(body, shape, dtype, args, flops):
    return pl.pallas_call(
        body,
        out_shape=pltpu.VMEM(shape, dtype),
        in_specs=[VMEM] * len(args),
        out_specs=VMEM,
        cost_estimate=pl.CostEstimate(flops=flops, bytes_accessed=sum(a.size * 2 for a in args), transcendentals=0),
        compiler_params=pltpu.CompilerParams(vmem_limit_bytes=8 << 20),
    )(*[pltpu.with_memory_space_constraint(a, pltpu.VMEM) for a in args])


def groups_of(n_pix):
    far = list(range(n_pix - 1, n_pix // 2 - 1, -1))
    return [list(range(n_pix // 2)), far[: len(far) // 2], far[len(far) // 2 :]]


def local(raw_frames, gain_map, coupling, factor_w, factor_h, n_scan, n_pix):
    scan_bits = n_scan.bit_length() - 1
    scan = lax.axis_index("scan")
    row_count, rank = factor_w.shape
    comp_rows, pixels = factor_h.shape
    half = rank // 2
    x_bits = [1 << b for b in range(1, scan_bits)]
    far = list(range(2, n_pix, 2))
    even = [0] + far
    odd = [r + 1 for r in even]
    scale = 1.0 / (pixels // 8)

    def over_pix(value, bit):
        return lax.ppermute(value, "pix", [(i, i ^ bit) for i in range(n_pix)])

    def over_scan(value, bit):
        return lax.ppermute(value, "scan", [(i, i ^ bit) for i in range(n_scan)])

    comp_order = [2 * j + c for c in range(2) for j in range(n_scan // 2)]
    back_order = [comp_order.index(j) for j in range(n_scan)]

    def to_global(w):
        at = [w[:, comp_rows * i : comp_rows * (i + 1)] for i in back_order]
        return jnp.concatenate(relative(at, scan), axis=1)

    w_local = reordered(factor_w, scan, comp_order)

    close = n_pix // 2
    frames = raw_frames.shape[0]
    tile = {r: [] for r in range(n_pix)}
    stencil = functools.partial(correct, raw_frames, gain_map, coupling, n_pix)
    early = stencil(True, 0, frames - 16)
    here = stencil(False, 0, frames, factor_w, comp_order)
    late = stencil(True, frames - 16, 16, factor_w, comp_order)
    tile[0].append(here[0])
    for first, messages in [(close, early), (0, here), (close, late)]:
        for i, message in enumerate(messages):
            r = first + i
            if r:
                tile[r].append(over_pix(message, r))

    for bit in x_bits:
        factor_h = jnp.concatenate([factor_h, over_scan(factor_h, bit)], 0)
    width = pixels // PARTS
    parts = [slice(width * c, width * (c + 1)) for c in range(PARTS)]
    h_mine = factor_h.astype(BF16)
    h_other = over_scan(h_mine, 1)
    h_own = [factor_h[:, part] for part in parts]
    h_pairs = [[h_mine[:, part], h_other[:, part]] for part in parts]

    def blocks(which):
        return [part for r in which for part in tile[r]]

    for rounds in range(ITERS):
        def ratio_of(values, w_round, pair):
            product = jnp.dot(w_round, jnp.concatenate(pair, axis=0), preferred_element_type=F32)
            return (values.astype(F32) / product).astype(BF16)

        def w_term(data, h_list, w=None):
            rows = sum(d.shape[0] for d in data)
            body = functools.partial(w_term_body, count=len(data), carried=w is None, scale=scale)
            args = [*data, *([] if w is None else [first_sums, w]), *h_list]
            return term(body, (rows + 16, rank), F32, args, 4 * rows * rank * pixels)

        def block_of(values, i):
            rows = values.shape[0] - 16
            return jnp.concatenate([values[row_count * i : row_count * (i + 1)], values[rows:]], axis=0)

        def combined(values, others):
            return functools.reduce(lambda a, b: a + b, [o.astype(F32) for o in others], values)

        if rounds == 0:
            backs, h_here = [], [h_mine, h_other]
            for group in groups_of(n_pix):
                partial = w_term(blocks(group), h_here)
                messages = {}
                for j, r in enumerate(group):
                    if r == 0:
                        numerator = block_of(partial, j)
                    else:
                        messages[r] = block_of(partial, j).astype(F16)
                h_here, messages = lax.optimization_barrier((h_here, messages))
                for r, message in messages.items():
                    backs.append(over_pix(message, r))
            numerator = combined(numerator, backs)
            h_sums = numerator[row_count : row_count + 1] + numerator[row_count + 1 : row_count + 2]
            first_sums = h_sums
            w_local = w_local * numerator[:row_count] / h_sums
        else:
            h_list = [h for pair in h_pairs for h in pair]
            back = over_pix(w_term([data_odd], h_list, w_odd).astype(F16), 1)
            near = w_term([data_even], h_list, w_even)
            near = combined(near, [back])
            backs = [over_pix(block_of(near, i + 1).astype(F16), r) for i, r in enumerate(far)]
            numerator = combined(block_of(near, 0), backs)
            h_sums = numerator[row_count : row_count + 1] + numerator[row_count + 1 : row_count + 2]
            w_local = w_local * (numerator[:row_count] + h_sums) / h_sums

        w_mine = w_local.astype(BF16)
        w_even = jnp.concatenate([w_mine] + [over_pix(w_mine, r) for r in far], axis=0)
        w_odd = over_pix(w_even, 1)
        if rounds == 0:
            shape = (row_count * len(even), pixels)
            data_even = term(tiles_body, shape, BF16, blocks(even), 0)
            data_odd = term(tiles_body, shape, BF16, blocks(odd), 0)

        def numerator_rows(w, ratio):
            return lax.dot_general(w, ratio, (((0,), (0,)), ((), ())), preferred_element_type=F32)

        last = rounds == ITERS - 1
        w_part = jnp.sum(w_even.astype(F32), axis=0) + jnp.sum(w_odd.astype(F32), axis=0)
        w_sums = w_part[:half] + over_scan(w_part[half:], 1)
        evens = []
        for part, pair in zip(parts, h_pairs):
            ratio = ratio_of(data_even[:, part], w_even, pair)
            evens.append([numerator_rows(w, ratio) for w in (w_even[:, :half], w_even[:, half:])])
        totals = []
        for c, (part, pair) in enumerate(zip(parts, h_pairs)):
            w_here = w_odd
            if c:
                w_here, _ = lax.optimization_barrier((w_odd, other))
            ratio = ratio_of(data_odd[:, part], w_here, pair)
            other = evens[c][1] + numerator_rows(w_here[:, half:], ratio)
            totals.append(evens[c][0] + numerator_rows(w_here[:, :half], ratio) + over_scan(other, 1))
        for bit in x_bits[::-1]:
            count = totals[0].shape[0] // comp_rows
            step = bit >> 1
            if last:
                keep = [i for i in range(count) if not i & step]
                send = [i | step for i in keep]
            else:
                keep = list(range(count))
                send = [i ^ step for i in keep]

            def pick(value, which):
                if list(which) == list(range(which[0], which[0] + len(which))):
                    return value[comp_rows * which[0] : comp_rows * (which[-1] + 1)]
                return jnp.concatenate([value[comp_rows * i : comp_rows * (i + 1)] for i in which], axis=0)

            sums = pick(w_sums, send)
            weight = over_scan(sums, bit)
            backs = []
            for c in range(PARTS):
                value = totals[c]
                if c:
                    value, _ = lax.optimization_barrier((value, message))
                message = (pick(value, send) / sums[:, None] - 1.0).astype(F16)
                backs.append(over_scan(message, bit))
            for c in range(PARTS):
                if c and bit == x_bits[0]:
                    backs[c], h_own[c - 1] = lax.optimization_barrier((backs[c], h_own[c - 1]))
                totals[c] = pick(totals[c], keep) + (backs[c].astype(F32) + 1.0) * weight[:, None]
                if bit == x_bits[0]:
                    h_own[c] = h_own[c][: totals[c].shape[0]] * totals[c] / (pick(w_sums, keep) + weight)[:, None]
                    if not last:
                        h_mine = h_own[c].astype(BF16)
                        h_pairs[c] = [h_mine, over_scan(h_mine, 1)]
            w_sums = pick(w_sums, keep) + weight
    return (to_global(w_local), jnp.concatenate(h_own, axis=1))


def solution(mesh):
    n_pix = mesh.shape["pix"]

    def layer(*args):
        return local(*args, n_scan=mesh.shape["scan"], n_pix=n_pix)

    return jax.shard_map(
        layer,
        mesh=mesh,
        in_specs=(
            P(("scan", "pix"), None, None),
            P(),
            P(),
            P(("scan", "pix"), None),
            P("scan", "pix"),
        ),
        out_specs=(P(("scan", "pix"), None), P("scan", "pix")),
        check_vma=False,
    )
```

```python
import functools

import jax
import jax.numpy as jnp
from jax import lax
from jax.experimental import pallas as pl
from jax.experimental.pallas import tpu as pltpu
from jax.sharding import PartitionSpec as P

SWEEPS = 4
ITERS = 2
BF16, F16, F32 = jnp.bfloat16, jnp.float16, jnp.float32


def relative(blocks, index):
    for bit in range(len(blocks).bit_length() - 1):
        flip = (index >> bit) & 1
        blocks = [jnp.where(flip == 1, blocks[j ^ (1 << bit)], blocks[j]) for j in range(len(blocks))]
    return blocks


def reordered(w, index, order):
    width = w.shape[1] // len(order)
    blocks = relative([w[:, width * j : width * (j + 1)] for j in range(len(order))], index)
    return jnp.concatenate([blocks[j] for j in order], axis=1)


def stencil_body(raw_ref, gain_ref, couple_ref, *refs, start, order, far):
    refs, (gain_s, near_s, stage) = refs[:-3], refs[-3:]
    rows, cols = gain_ref.shape
    parts, frames, pixels = stage.shape
    groups = frames // 8
    band = rows // (2 * parts)
    me = lax.axis_index("pix")
    own_half = me // parts
    half = 1 - own_half if far else own_half
    first_row = half * (rows // 2)
    above = half.astype(F32)
    below = 1.0 - above

    @pl.when(pl.program_id(0) == 0)
    def _():
        inverse = 1.0 / (1.0 + 4.0 * couple_ref[...])
        gain_s[...] = gain_ref[...] * inverse
        near_s[...] = couple_ref[...] * inverse

    lane = lax.broadcasted_iota(jnp.int32, (8, cols), 1)
    has_left = jnp.where(lane == 0, 0.0, 1.0)
    has_right = jnp.where(lane == cols - 1, 0.0, 1.0)
    zero = jnp.zeros((8, cols), F32)

    def every(ref, row):
        return ref[pl.ds(row, 8, stride=0), :]

    def advance(state, row, there=None):
        levels, scaled, weight = state
        w_new = every(near_s, row)
        gain = every(gain_ref, row)
        gain_scaled = every(gain_s, row)
        if there is not None:
            w_new, gain, gain_scaled = w_new * there, gain * there, gain_scaled * there
        raws = [raw_ref[pl.ds(g * 8 * rows + row, 8, stride=rows), :] for g in range(groups)]
        enter = [raw * gain for raw in raws]
        s_new = [raw * gain_scaled for raw in raws]
        out, new_levels = [], []
        for g in range(groups):
            new = enter[g]
            mine = []
            for k in range(SWEEPS):
                older, newer = levels[g][k]
                side = pltpu.roll(newer, 1, 1) * has_left + pltpu.roll(newer, cols - 1, 1) * has_right
                value = scaled[g][k] + weight[k] * ((older + side) + new)
                mine.append((newer, new))
                new = value
            out.append(new)
            new_levels.append(mine)
        scaled = [[s_new[g]] + scaled[g][: SWEEPS - 1] for g in range(groups)]
        return (new_levels, scaled, [w_new] + weight[: SWEEPS - 1]), out

    frame = lax.broadcasted_iota(jnp.int32, (frames, cols), 0) + frames * pl.program_id(0) + start
    phase = frame.astype(F32) * 0.6180340 + lax.broadcasted_iota(jnp.int32, (frames, cols), 1).astype(F32) * 0.7548777
    shift = (phase - jnp.floor(phase) - 0.5) * 0.005

    def one_band(part, state, error, first=False, last=False):
        for i in range(band):
            if last and i + SWEEPS >= band:
                row = jnp.minimum(first_row + rows // 2 + (i + SWEEPS - band), rows - 1)
                state, out = advance(state, row, below)
            else:
                state, out = advance(state, first_row + part * band + SWEEPS + i)
            value = jnp.concatenate(out, axis=0)
            value = value + (value * shift if first and i == 0 else error)
            rounded = value.astype(BF16)
            error = value - rounded.astype(F32)
            stage[part, :, i * cols : (i + 1) * cols] = rounded
        return state, error

    state = (
        [[(zero, zero)] * SWEEPS for _ in range(groups)],
        [[zero] * SWEEPS for _ in range(groups)],
        [zero] * SWEEPS,
    )
    for i in range(SWEEPS):
        state, _ = advance(state, jnp.maximum(first_row - SWEEPS + i, 0), above)
    for i in range(SWEEPS):
        state, _ = advance(state, first_row + i)
    carry = one_band(0, state, None, first=True)
    carry = lax.fori_loop(1, parts - 1, lambda part, c: one_band(part, *c), carry)
    one_band(parts - 1, *carry, last=True)
    w = None
    if order is not None:
        w, refs = reordered(refs[0][...], lax.axis_index("scan"), order).astype(BF16), refs[1:]
    for r, out_ref in enumerate(refs):
        out_ref[:, :pixels] = stage[jnp.bitwise_xor(me, r) % parts]
        for i in range(0 if w is None else w.shape[0] // frames):
            at, rank = pixels + w.shape[1] * i, w.shape[1]
            out_ref[:, at : at + rank] = w[frames * i : frames * (i + 1)]


def correct(raw_frames, gain_map, coupling, parts, far, start, count, factor_w=None, order=None):
    frames, rows, cols = raw_frames.shape
    group = 16
    pixels = rows * cols // parts
    first = start // group
    extra, specs, width = [], [], pixels
    if factor_w is not None:
        rank = factor_w.shape[1]
        extra = [factor_w]
        if count == frames:
            specs, width = [pl.BlockSpec((group, rank), lambda i: (i, 0))], pixels + rank
        else:
            specs, width = [pl.BlockSpec((frames, rank), lambda i: (0, 0))], pixels + rank * (frames // group)
    return pl.pallas_call(
        functools.partial(stencil_body, start=start, order=order, far=far),
        out_shape=[jax.ShapeDtypeStruct((count, width), BF16)] * (parts // 2),
        grid_spec=pl.GridSpec(
            grid=(count // group,),
            in_specs=[
                pl.BlockSpec((group * rows, cols), lambda i: (i + first, 0)),
                pl.BlockSpec((rows, cols), lambda i: (0, 0)),
                pl.BlockSpec((rows, cols), lambda i: (0, 0)),
            ]
            + specs,
            out_specs=[pl.BlockSpec((group, width), lambda i: (i, 0))] * (parts // 2),
            scratch_shapes=[pltpu.VMEM((rows, cols), F32)] * 2 + [pltpu.VMEM((parts // 2, group, pixels), BF16)],
        ),
        cost_estimate=pl.CostEstimate(
            flops=count * rows * cols * SWEEPS * 5,
            bytes_accessed=count * rows * cols * 5,
            transcendentals=0,
        ),
        name="charge_sharing",
    )(raw_frames.reshape(frames * rows, cols), gain_map, coupling, *extra)


TILE = 512
PARTS = 2


def w_term_body(*refs, count, carried, scale):
    out_ref = refs[-1]
    data_refs, rest = refs[:count], list(refs[count:-1])
    rank = out_ref.shape[1]
    rows = sum(ref.shape[0] for ref in data_refs)
    by = None if carried else rest.pop(0)[...]
    w_ref = None if carried else rest.pop(0)
    pixels = sum(ref.shape[1] for ref in rest[::2])
    if carried:
        w = jnp.concatenate([ref[:, at : at + rank] for ref in data_refs for at in range(pixels, ref.shape[1], rank)], axis=0)
    else:
        w = w_ref[...]
    total, start = None, 0
    for pair in zip(rest[::2], rest[1::2]):
        width = pair[0].shape[1]
        tile = min(TILE, width)
        ones = jnp.ones((16, tile), BF16)
        for at in range(0, width, tile):
            h_tile = jnp.concatenate([ref[:, at : at + tile] for ref in pair], axis=0)
            product = jnp.dot(w, h_tile, preferred_element_type=F32)
            values = jnp.concatenate([ref[:, start + at : start + at + tile] for ref in data_refs], axis=0).astype(F32)
            ratio = jnp.concatenate([(values / product).astype(BF16), ones], axis=0)
            term = lax.dot_general(ratio, h_tile, (((1,), (1,)), ((), ())), preferred_element_type=F32)
            total = term if total is None else total + term
        start += width
    sums = total[rows : rows + 1]
    if carried:
        numerators, sums = total[:rows] * scale, sums * scale
    else:
        numerators, sums = (total[:rows] - sums) / by, sums / by
    high = sums.astype(BF16).astype(F32)
    line = lax.broadcasted_iota(jnp.int32, (16, rank), 0)
    out_ref[:rows] = numerators
    out_ref[rows:] = jnp.where(line == 0, high, jnp.where(line == 1, sums - high, 0.0))


def tiles_body(*refs):
    *data_refs, out_ref = refs
    pixels = out_ref.shape[1]
    row = 0
    for ref in data_refs:
        out_ref[row : row + ref.shape[0], :] = ref[:, :pixels]
        row += ref.shape[0]


VMEM = pl.BlockSpec(memory_space=pltpu.VMEM)


def term(body, shape, dtype, args, flops):
    return pl.pallas_call(
        body,
        out_shape=pltpu.VMEM(shape, dtype),
        in_specs=[VMEM] * len(args),
        out_specs=VMEM,
        cost_estimate=pl.CostEstimate(flops=flops, bytes_accessed=sum(a.size * 2 for a in args), transcendentals=0),
        compiler_params=pltpu.CompilerParams(vmem_limit_bytes=8 << 20),
    )(*[pltpu.with_memory_space_constraint(a, pltpu.VMEM) for a in args])


def groups_of(n_pix):
    far = list(range(n_pix - 1, n_pix // 2 - 1, -1))
    return [list(range(n_pix // 2)), far]


def local(raw_frames, gain_map, coupling, factor_w, factor_h, n_scan, n_pix):
    scan_bits = n_scan.bit_length() - 1
    scan = lax.axis_index("scan")
    row_count, rank = factor_w.shape
    comp_rows, pixels = factor_h.shape
    half = rank // 2
    x_bits = [1 << b for b in range(1, scan_bits)]
    far = list(range(2, n_pix, 2))
    even = [0] + far
    odd = [r + 1 for r in even]
    scale = 1.0 / (pixels // 8)

    def over_pix(value, bit):
        return lax.ppermute(value, "pix", [(i, i ^ bit) for i in range(n_pix)])

    def over_scan(value, bit):
        return lax.ppermute(value, "scan", [(i, i ^ bit) for i in range(n_scan)])

    comp_order = [2 * j + c for c in range(2) for j in range(n_scan // 2)]
    back_order = [comp_order.index(j) for j in range(n_scan)]

    def to_global(w):
        at = [w[:, comp_rows * i : comp_rows * (i + 1)] for i in back_order]
        return jnp.concatenate(relative(at, scan), axis=1)

    w_local = reordered(factor_w, scan, comp_order)

    close = n_pix // 2
    frames = raw_frames.shape[0]
    tile = {r: [] for r in range(n_pix)}
    stencil = functools.partial(correct, raw_frames, gain_map, coupling, n_pix)
    early = stencil(True, 0, frames - 16)
    here = stencil(False, 0, frames, factor_w, comp_order)
    late = stencil(True, frames - 16, 16, factor_w, comp_order)
    tile[0].append(here[0])
    for first, messages in [(close, early), (0, here), (close, late)]:
        for i, message in enumerate(messages):
            r = first + i
            if r:
                tile[r].append(over_pix(message, r))

    for bit in x_bits:
        factor_h = jnp.concatenate([factor_h, over_scan(factor_h, bit)], 0)
    width = pixels // PARTS
    parts = [slice(width * c, width * (c + 1)) for c in range(PARTS)]
    h_mine = factor_h.astype(BF16)
    h_other = over_scan(h_mine, 1)
    h_own = [factor_h[:, part] for part in parts]
    h_pairs = [[h_mine[:, part], h_other[:, part]] for part in parts]

    def blocks(which):
        return [part for r in which for part in tile[r]]

    for rounds in range(ITERS):
        def ratio_of(values, w_round, pair):
            product = jnp.dot(w_round, jnp.concatenate(pair, axis=0), preferred_element_type=F32)
            return (values.astype(F32) / product).astype(BF16)

        def w_term(data, h_list, w=None):
            rows = sum(d.shape[0] for d in data)
            body = functools.partial(w_term_body, count=len(data), carried=w is None, scale=scale)
            args = [*data, *([] if w is None else [first_sums, w]), *h_list]
            return term(body, (rows + 16, rank), F32, args, 4 * rows * rank * pixels)

        def block_of(values, i):
            rows = values.shape[0] - 16
            return jnp.concatenate([values[row_count * i : row_count * (i + 1)], values[rows:]], axis=0)

        def combined(values, others):
            return functools.reduce(lambda a, b: a + b, [o.astype(F32) for o in others], values)

        if rounds == 0:
            backs, h_here = [], [h_mine, h_other]
            for group in groups_of(n_pix):
                partial = w_term(blocks(group), h_here)
                messages = {}
                for j, r in enumerate(group):
                    if r == 0:
                        numerator = block_of(partial, j)
                    else:
                        messages[r] = block_of(partial, j).astype(F16)
                h_here, messages = lax.optimization_barrier((h_here, messages))
                for r, message in messages.items():
                    backs.append(over_pix(message, r))
            numerator = combined(numerator, backs)
            h_sums = numerator[row_count : row_count + 1] + numerator[row_count + 1 : row_count + 2]
            first_sums = h_sums
            w_local = w_local * numerator[:row_count] / h_sums
        else:
            h_list = [h for pair in h_pairs for h in pair]
            back = over_pix(w_term([data_odd], h_list, w_odd).astype(F16), 1)
            near = w_term([data_even], h_list, w_even)
            near = combined(near, [back])
            backs = [over_pix(block_of(near, i + 1).astype(F16), r) for i, r in enumerate(far)]
            numerator = combined(block_of(near, 0), backs)
            h_sums = numerator[row_count : row_count + 1] + numerator[row_count + 1 : row_count + 2]
            w_local = w_local * (numerator[:row_count] + h_sums) / h_sums

        w_mine = w_local.astype(BF16)
        w_even = jnp.concatenate([w_mine] + [over_pix(w_mine, r) for r in far], axis=0)
        w_odd = over_pix(w_even, 1)
        if rounds == 0:
            shape = (row_count * len(even), pixels)
            data_even = term(tiles_body, shape, BF16, blocks(even), 0)
            data_odd = term(tiles_body, shape, BF16, blocks(odd), 0)

        def numerator_rows(w, ratio):
            return lax.dot_general(w, ratio, (((0,), (0,)), ((), ())), preferred_element_type=F32)

        last = rounds == ITERS - 1
        w_part = jnp.sum(w_even.astype(F32), axis=0) + jnp.sum(w_odd.astype(F32), axis=0)
        w_sums = w_part[:half] + over_scan(w_part[half:], 1)
        evens = []
        for part, pair in zip(parts, h_pairs):
            ratio = ratio_of(data_even[:, part], w_even, pair)
            evens.append([numerator_rows(w, ratio) for w in (w_even[:, :half], w_even[:, half:])])
        totals = []
        for c, (part, pair) in enumerate(zip(parts, h_pairs)):
            w_here = w_odd
            if c:
                w_here, _ = lax.optimization_barrier((w_odd, other))
            ratio = ratio_of(data_odd[:, part], w_here, pair)
            other = evens[c][1] + numerator_rows(w_here[:, half:], ratio)
            totals.append(evens[c][0] + numerator_rows(w_here[:, :half], ratio) + over_scan(other, 1))
        for bit in x_bits[::-1]:
            count = totals[0].shape[0] // comp_rows
            step = bit >> 1
            if last:
                keep = [i for i in range(count) if not i & step]
                send = [i | step for i in keep]
            else:
                keep = list(range(count))
                send = [i ^ step for i in keep]

            def pick(value, which):
                if list(which) == list(range(which[0], which[0] + len(which))):
                    return value[comp_rows * which[0] : comp_rows * (which[-1] + 1)]
                return jnp.concatenate([value[comp_rows * i : comp_rows * (i + 1)] for i in which], axis=0)

            sums = pick(w_sums, send)
            weight = over_scan(sums, bit)
            backs = []
            for c in range(PARTS):
                value = totals[c]
                if c:
                    value, _ = lax.optimization_barrier((value, message))
                message = (pick(value, send) / sums[:, None] - 1.0).astype(F16)
                backs.append(over_scan(message, bit))
            for c in range(PARTS):
                if c and bit == x_bits[0]:
                    backs[c], h_own[c - 1] = lax.optimization_barrier((backs[c], h_own[c - 1]))
                totals[c] = pick(totals[c], keep) + (backs[c].astype(F32) + 1.0) * weight[:, None]
                if bit == x_bits[0]:
                    h_own[c] = h_own[c][: totals[c].shape[0]] * totals[c] / (pick(w_sums, keep) + weight)[:, None]
                    if not last:
                        h_mine = h_own[c].astype(BF16)
                        h_pairs[c] = [h_mine, over_scan(h_mine, 1)]
            w_sums = pick(w_sums, keep) + weight
    w_factor = to_global(w_local)
    return (w_factor, jnp.concatenate(h_own, axis=1))


def solution(mesh):
    n_pix = mesh.shape["pix"]

    def layer(*args):
        return local(*args, n_scan=mesh.shape["scan"], n_pix=n_pix)

    return jax.shard_map(
        layer,
        mesh=mesh,
        in_specs=(
            P(("scan", "pix"), None, None),
            P(),
            P(),
            P(("scan", "pix"), None),
            P("scan", "pix"),
        ),
        out_specs=(P(("scan", "pix"), None), P("scan", "pix")),
        check_vma=False,
    )
```
